512 devices in a mesh: seq: 16 (over z), head: 32 (over x, y, core).
Axes of the slice: x: 4, y: 4, z: 16, core: 2. Of those that a mesh axis runs over, the one named last changes fastest.
Arguments:
- queries: bfloat16 [32768, 8192], P('seq', 'head'), may hold values from -6 to 6
- key_rows: bfloat16 [32768, 8192], P('seq', 'head'), may hold values from -0.52734375 to 0.52734375
- value_rows: bfloat16 [32768, 8192], P('seq', 'head')
- log_decay: float32 [64, 32768], P('head', 'seq')
- norm_gain: float32 [8192], P('head'), may hold values from 0.1 to 1.9
- lengths: int32 [48], replicated, may hold values from 1 to 4095, as said below
- decode_slot: int32 [48], replicated, may hold values from 0 to 47, each once
Outputs:
- attended: bfloat16 [32768, 8192], P('seq', 'head')
- final_states: float32 [48, 64, 128, 128], P('seq', 'head')
The draws below stay inside these ranges and needn't reach their ends.
Inputs may be any that keep to these rules, and one draw needn't show every extreme that they name: The lengths sum to 32768. Every block of 2048 consecutive positions (one index of seq) holds between 1 and 5 last positions of prompts; the last position of the pack ends a prompt; in every draw some block holds 5 and some holds 1. `decode_slot`: each row of final_states is named once; rows j * 3 to j * 3 + 2 lie on index j of seq.
All inputs are finite; a program needn't handle non-finite values.
Results may differ from the reference program's by a relative error of at most 0.0075.
Values sent between devices are 32-bit elements; how exact they have to be, the bound alone decides.
A program may use at most 64 MiB of HBM per device.

```python
import math
import jax
import jax.numpy as jnp
from jax import lax

DK = 128
DV = 128
TOK_DEV = 2048
BLK = 1024
SLOTS = 3
HEADS = 64
PACKED_TOKENS = 32768
PROMPTS = 48
ENDS = 5


def draw_value_rows(key, part):
    random_subkeys = jax.random.split(key, 2)
    head_pos = jnp.arange(HEADS, dtype=jnp.float32) / max(HEADS - 1, 1)
    jitter = jnp.exp(jax.random.uniform(random_subkeys[0], (HEADS,), jnp.float32, math.log(0.9), math.log(1.1)))
    base = jax.random.normal(random_subkeys[1], (PACKED_TOKENS, HEADS, DV), jnp.float32)
    rising = (1.0 + 3.0 * head_pos) * jitter
    return (base * rising[None, :, None]).reshape(PACKED_TOKENS, HEADS * DV).astype(jnp.bfloat16)


def draw_log_decay(key, part):
    random_subkeys = jax.random.split(key, 7)
    slow_rate = jnp.exp(jax.random.uniform(random_subkeys[0], (HEADS,), jnp.float32, math.log(0.05), math.log(0.5))) / (2.0 * TOK_DEV)
    fast_rate = jnp.exp(jax.random.uniform(random_subkeys[1], (HEADS,), jnp.float32, math.log(20.0), math.log(34.0))) / BLK
    fast_share = 0.5
    fast_flag = jax.random.uniform(random_subkeys[2], (HEADS,), jnp.float32) < fast_share
    head_decay_rate = jnp.where(fast_flag, fast_rate, slow_rate)
    token_decay_factor = jax.random.uniform(random_subkeys[3], (HEADS, PACKED_TOKENS), jnp.float32, 0.5, 2.0)
    block_decay_factor = jnp.repeat(jax.random.uniform(random_subkeys[4], (HEADS, PACKED_TOKENS // BLK), jnp.float32, 0.5, 2.0), BLK, axis=1)
    spike_position = jax.random.uniform(random_subkeys[5], (PACKED_TOKENS,), jnp.float32) < 8.0 / PACKED_TOKENS
    spike_log_decay = jnp.log(jax.random.uniform(random_subkeys[6], (PACKED_TOKENS,), jnp.float32, 0.5, 0.8))
    return -head_decay_rate[:, None] * token_decay_factor * block_decay_factor + jnp.where(spike_position, spike_log_decay, 0.0)[None, :]


def draw_lengths(key, part):
    random_subkeys = jax.random.split(key, 4)
    device_count = PACKED_TOKENS // TOK_DEV
    pair_count = device_count // 2
    shift_amount = jax.random.randint(random_subkeys[1], (pair_count,), 0, SLOTS)
    shift_amount = shift_amount.at[0].set(SLOTS - 1).at[1].set(SLOTS - 1)
    pair_values = jnp.stack([SLOTS + shift_amount, SLOTS - shift_amount], axis=1).reshape(device_count).astype(jnp.int32)
    rest_values = jnp.concatenate([pair_values[0:1], pair_values[2:3], pair_values[4:]])
    later_dev = jax.random.randint(random_subkeys[3], (), 1, device_count).astype(jnp.int32)
    earlier_dev = later_dev - 1
    other_index = jnp.arange(device_count - 2, dtype=jnp.int32)
    other_devs = jnp.where(other_index < earlier_dev, other_index, other_index + 2)
    other_order = jax.random.permutation(random_subkeys[0], device_count - 2)
    end_counts = jnp.zeros((device_count,), jnp.int32).at[other_devs[other_order]].set(rest_values)
    end_counts = end_counts.at[earlier_dev].set(1).at[later_dev].set(1)
    device_keys = jax.random.split(random_subkeys[2], device_count)
    shuffled = jax.vmap(lambda sub_key: jax.random.permutation(sub_key, TOK_DEV - 1))(device_keys)
    candidate = shuffled[:, :ENDS].astype(jnp.int32)
    candidate = candidate.at[earlier_dev, 0].set(0)
    candidate = candidate.at[later_dev, 0].set(TOK_DEV - 1)
    candidate = candidate.at[device_count - 1, 0].set(TOK_DEV - 1)
    is_valid = jnp.arange(ENDS, dtype=jnp.int32)[None, :] < end_counts[:, None]
    global_pos = jnp.arange(device_count, dtype=jnp.int32)[:, None] * TOK_DEV + candidate
    global_pos = jnp.where(is_valid, global_pos, 2 * PACKED_TOKENS)
    end_pos = jnp.sort(global_pos.reshape(-1))[:device_count * SLOTS]
    before_pos = jnp.concatenate([jnp.full((1,), -1, jnp.int32), end_pos[:-1]])
    return (end_pos - before_pos).astype(jnp.int32)


def steps_of(key, shape, cuts, least, largest):
    def one(dim, parts):
        heights = jax.random.uniform(jax.random.fold_in(jax.random.fold_in(key, 6), dim), (parts,), jnp.float32, least / len(cuts), largest / len(cuts))
        return jnp.repeat(jnp.exp(heights), shape[dim] // parts).reshape((-1,) + (1,) * (len(shape) - dim - 1))

    loudness = one(*cuts[0])
    for cut in cuts[1:]:
        loudness = loudness * one(*cut)
    return loudness


def scatter_about(rng, extent, deviation, most, cuts=(), kind=jnp.bfloat16):
    values = deviation * jax.random.normal(rng, extent, jnp.float32)
    if cuts:
        values = values * steps_of(rng, extent, cuts, -0.22, 0.18)
    return jnp.clip(values, -most, most).astype(kind)


def setup_inputs(seed: int = 0) -> dict:
    key_of = jax.random.split(jax.random.key(seed), 8)
    queries = scatter_about(key_of[0], (PACKED_TOKENS, HEADS * DK), 1.0, 6.0, ((0, 16), (1, 32)))
    key_rows = scatter_about(key_of[1], (PACKED_TOKENS, HEADS * DK), (DK ** -0.5), 0.52734375, ((0, 16), (1, 32)))
    value_rows = draw_value_rows(jax.random.fold_in(key_of[7], 71), 0)
    log_decay = draw_log_decay(jax.random.fold_in(key_of[7], 71), 0)
    norm_gain = jnp.clip(1.0 + 0.18 * jax.random.normal(key_of[4], (HEADS * DV,), jnp.float32), 0.1, 1.9)
    lengths = draw_lengths(jax.random.fold_in(key_of[7], 71), 0)
    decode_slot = jax.random.permutation(key_of[6], PROMPTS).astype(jnp.int32)
    return {"queries": queries, "key_rows": key_rows, "value_rows": value_rows, "log_decay": log_decay, "norm_gain": norm_gain, "lengths": lengths, "decode_slot": decode_slot}


precise = lax.Precision.HIGHEST
epsilon = 1e-06

def segment_of(lengths, positions):
    finish = jnp.cumsum(lengths)
    begins = finish - lengths
    return lax.optimization_barrier(jnp.sum((begins[None, :] <= positions[:, None]).astype(jnp.int32), axis=1)) - 1

def reference(queries, key_rows, value_rows, log_decay, norm_gain, lengths, decode_slot):
    head_count = log_decay.shape[0]
    block_count = PACKED_TOKENS // BLK
    positions = jnp.arange(PACKED_TOKENS, dtype=jnp.int32)
    segment = segment_of(lengths, positions)
    previous = jnp.concatenate([jnp.full((1,), -1, jnp.int32), segment[:-1]])
    query_blocks = queries.reshape(block_count, BLK, head_count, DK)
    key_blocks = key_rows.reshape(block_count, BLK, head_count, DK)
    value_blocks = value_rows.reshape(block_count, BLK, head_count, DV)
    decay_blocks = log_decay.reshape(head_count, block_count, BLK).transpose(1, 0, 2)
    segment_blocks = segment.reshape(block_count, BLK)
    entry_blocks = previous.reshape(block_count, BLK)[:, 0]
    causal = jnp.arange(BLK, dtype=jnp.int32)[:, None] >= jnp.arange(BLK, dtype=jnp.int32)[None, :]

    def one_block(carry_state, inputs):
        query_blk, key_blk, value_blk, decay_blk, seg_blk, entry_seg = inputs
        running = jnp.cumsum(decay_blk, axis=1)
        same_seg = ((seg_blk[:, None] == seg_blk[None, :]) & causal)[None]
        gap_log = jnp.where(same_seg, running[:, :, None] - running[:, None, :], 0.0)
        weight = jnp.where(same_seg, jnp.exp(gap_log), 0.0)
        scores = jnp.einsum('ihd,jhd->hij', query_blk.astype(jnp.float32), key_blk.astype(jnp.float32))
        weights_bf = (scores * weight).astype(jnp.bfloat16)
        inside_out = jnp.einsum('hij,jhe->ihe', weights_bf.astype(jnp.float32), value_blk.astype(jnp.float32))
        reach = jnp.where((seg_blk == entry_seg)[None, :], jnp.exp(running), 0.0)
        through = jnp.einsum('ihd,hde->ihe', query_blk.astype(jnp.float32), carry_state, precision=precise)
        mixed = inside_out + through * reach.T[:, :, None]
        last_seg = seg_blk[BLK - 1]
        tail_member = (seg_blk == last_seg)[None, :]
        tail_weight = jnp.where(tail_member, jnp.exp(running[:, BLK - 1:] - running), 0.0)
        block_state = jnp.einsum('hj,jhd,jhe->hde', tail_weight, key_blk.astype(jnp.float32), value_blk.astype(jnp.float32), precision=precise)
        keep_factor = jnp.where(last_seg == entry_seg, jnp.exp(running[:, BLK - 1]), 0.0)
        return (keep_factor[:, None, None] * carry_state + block_state, (mixed, carry_state))
    start_state = jnp.zeros((head_count, DK, DV), jnp.float32)
    final_carry, outputs = lax.scan(one_block, start_state, (query_blocks, key_blocks, value_blocks, decay_blocks, segment_blocks, entry_blocks))
    mixed_all, states_before = outputs
    mixed_rows = mixed_all.reshape(PACKED_TOKENS, head_count * DV)
    mean_sq = lax.optimization_barrier(jnp.mean(mixed_rows * mixed_rows, axis=1, keepdims=True))
    attended = (mixed_rows * lax.rsqrt(mean_sq + epsilon) * norm_gain[None, :]).astype(jnp.bfloat16)
    finish_pos = (jnp.cumsum(lengths) - 1).astype(jnp.int32)

    def end_state(end_pos):
        block_index = (end_pos // BLK).astype(jnp.int32)
        start = (block_index * BLK).astype(jnp.int32)
        key_blk = lax.dynamic_slice_in_dim(key_rows, start, BLK, 0).reshape(BLK, head_count, DK).astype(jnp.float32)
        value_blk = lax.dynamic_slice_in_dim(value_rows, start, BLK, 0).reshape(BLK, head_count, DV).astype(jnp.float32)
        decay_blk = lax.dynamic_slice_in_dim(log_decay, start, BLK, 1)
        seg_blk = lax.dynamic_slice_in_dim(segment, start, BLK, 0)
        running = jnp.cumsum(decay_blk, axis=1)
        offset = (end_pos - start).astype(jnp.int32)
        running_end = lax.dynamic_slice_in_dim(running, offset, 1, 1)
        target = lax.dynamic_slice_in_dim(segment, end_pos, 1, 0)[0]
        member = (seg_blk == target)[None, :]
        weight = jnp.where(member, jnp.exp(jnp.where(member, running_end - running, 0.0)), 0.0)
        inside = jnp.einsum('hj,jhd,jhe->hde', weight, key_blk, value_blk, precision=precise)
        entry_seg = lax.dynamic_slice_in_dim(previous, start, 1, 0)[0]
        carry_in = jnp.where(target == entry_seg, jnp.exp(running_end[:, 0]), 0.0)
        before = lax.dynamic_index_in_dim(states_before, block_index, 0, keepdims=False)
        return carry_in[:, None, None] * before + inside
    ended = lax.map(end_state, finish_pos)
    final_states = jnp.zeros_like(ended).at[decode_slot].set(ended)
    return (attended, final_states)
```

```python
import functools

import jax
import jax.numpy as jnp
from jax import lax
from jax.experimental import pallas as pl
from jax.experimental.pallas import tpu as pltpu
from jax.sharding import PartitionSpec as P

DK = 128
DV = 128
CHUNK = 256
SLOTS = 3
ENDS = 5
LANES = 128
LONGEST = 32
LENGTHS = (9, 10, 11, 12, 13, 14, 16, 18, 21, LONGEST)
FAR = 1 << 20
NEG = -1e30
EPSILON = 1e-06
MESH = pl.DeviceIdType.MESH
F32 = jnp.float32
BF16 = jnp.bfloat16
SORT5 = ((0, 1), (3, 4), (2, 4), (2, 3), (1, 4), (0, 3), (0, 2), (1, 3), (1, 2))
PRECISE = lax.Precision.HIGHEST


def iota(shape, axis):
    return lax.broadcasted_iota(jnp.int32, shape, axis)


def halves(wide, axis):
    upper = wide.astype(BF16)
    lower = (wide - upper.astype(F32)).astype(BF16)
    return jnp.concatenate([upper, lower], axis=axis)


def outer_sum(scaled_keys, values):
    both = lax.dot_general(
        halves(scaled_keys, 1), values, (((0,), (0,)), ((), ())), preferred_element_type=F32
    )
    return both[:DK] + both[DK:]


def query_state(rows, state_halves):
    both = jnp.dot(rows, state_halves, preferred_element_type=F32)
    return both[:, :DV] + both[:, DV:]


def route(me, ring, tok, prompts, finish, slot_ref):
    shape = (8, LANES)
    sub, place = iota(shape, 0), iota(shape, 1) & (ring - 1)
    dev = jnp.where(sub == 0, place, (ring - place) & (ring - 1))
    start = dev * tok
    first = jnp.zeros(shape, jnp.int32)
    for p in range(prompts):
        first = first + jnp.where(finish[p] < start, 1, 0)
    items = [jnp.zeros(shape, jnp.int32)] * ENDS
    for p in range(prompts):
        slot = slot_ref[p]
        owner = (slot * 43) >> 7
        value = owner * 4 + (slot - owner * SLOTS) + 1
        here = (finish[p] >= start) & (finish[p] < start + tok)
        rank = jnp.where(here, p - first, -1)
        items = [jnp.where(rank == k, value, item) for k, item in enumerate(items)]
    keys, own = [], []
    for k, item in enumerate(items):
        owner, row = (item - 1) >> 2, (item - 1) & 3
        right = (owner - dev) & (ring - 1)
        left = (ring - right) & (ring - 1)
        go_right = (right < ring // 2) | ((right == ring // 2) & (((dev + k) & 1) == 0))
        on_right = (sub == 0) & go_right
        on_left = (sub == 1) & jnp.logical_not(go_right)
        chosen = (item > 0) & (right > 0) & (on_right | on_left)
        distance = jnp.where(sub == 0, right, left)
        keys.append(jnp.where(chosen, distance * 64 + k * 8 + row, 0))
        own.append(jnp.where((item > 0) & (right == 0), row + 1, 0))
    for a, b in SORT5:
        keys[a], keys[b] = jnp.maximum(keys[a], keys[b]), jnp.minimum(keys[a], keys[b])
    lane = iota(shape, 1)
    mine = ((sub == 0) & (lane == me)) | ((sub == 1) & (lane == ((ring - me) & (ring - 1))))
    belt = jnp.zeros(shape, jnp.int32)
    last = jnp.zeros(shape, jnp.int32)
    boards, takes = [], []
    for t in range(LONGEST):
        board = (belt == 0) & (keys[0] > 0)
        boards.append(jnp.where(board & mine, ((keys[0] >> 3) & 7) + 1, 0))
        belt = jnp.where(board, keys[0], belt)
        following = keys[1:] + [jnp.zeros(shape, jnp.int32)]
        keys = [jnp.where(board, new, old) for new, old in zip(following, keys)]
        last = jnp.where(belt > 0, t + 1, last)
        moved = jnp.where(belt >= 128, belt - 64, jnp.where(belt >= 64, (belt & 7) + 1, 0))
        moved = pltpu.roll(moved, 1, 1)
        takes.append(jnp.where(mine & (moved < 64), moved, 0))
        belt = jnp.where(moved >= 64, moved, 0)
    own = [jnp.where(mine & (sub == 0), item, 0) for item in own]
    tiles = boards + takes + own + [jnp.zeros(shape, jnp.int32)]
    stacked = jnp.concatenate(tiles, axis=0).astype(F32).astype(BF16)
    table = jnp.dot(stacked, jnp.ones((LANES, LANES), BF16), preferred_element_type=F32)
    return table, jnp.max(last)


def local_kernel(
    ring,
    len_ref,
    slot_ref,
    decay_ref,
    q_ref,
    k_ref,
    v_ref,
    out_ref,
    reached_ref,
    ends_ref,
    tail_ref,
    table_ref,
    first_ref,
    branch_ref,
    run_row,
    run_col,
    state,
    finish_s,
):
    tok = q_ref.shape[0]
    heads = decay_ref.shape[0]
    prompts = len_ref.shape[0]
    tiles = tok // LANES
    me = lax.axis_index("seq")
    anchor = me * tok

    decay = decay_ref[...]
    rows = jnp.concatenate(
        [decay[:, c * LANES : (c + 1) * LANES] for c in range(tiles)], axis=0
    )
    square = (LANES, LANES)
    upper = (iota(square, 0) <= iota(square, 1)).astype(F32)
    within = jnp.dot(rows, upper, precision=PRECISE, preferred_element_type=F32)
    count = tiles * heads
    wide = jnp.concatenate([within, jnp.zeros((LANES - count, LANES), F32)], axis=0)
    totals = jnp.broadcast_to(wide[:, LANES - 1 :], square)
    earlier = (iota(square, 1) < iota(square, 0)) & (
        ((iota(square, 0) - iota(square, 1)) & (heads - 1)) == 0
    )
    running = wide + jnp.dot(
        earlier.astype(F32), totals, precision=PRECISE, preferred_element_type=F32
    )
    run_row[...] = running
    turned = running.T
    for c in range(tiles):
        shift = (LANES - heads * c) % LANES
        run_col[c * LANES : (c + 1) * LANES, :] = (
            pltpu.roll(turned, shift, 1) if shift else turned
        )

    total = jnp.int32(0)
    before = jnp.int32(0)
    ended = jnp.int32(0)
    finish = []
    for p in range(prompts):
        total = total + len_ref[p]
        finish.append(total - 1)
        finish_s[p] = total - 1
        before = before + jnp.where(total - 1 < anchor, 1, 0)
        ended = ended + jnp.where(total - 1 < anchor + tok, 1, 0)
    ended = ended - before
    ends = []
    for k in range(ENDS):
        place = finish_s[jnp.minimum(before + k, prompts - 1)] - anchor
        ends.append(jnp.where(k < ended, place, FAR))

    table, steps = route(me, ring, tok, prompts, finish, slot_ref)
    table_ref[...] = table
    branch = jnp.int32(0)
    for length in LENGTHS[:-1]:
        branch = branch + jnp.where(steps > length, 1, 0)
    branch_ref[0] = branch

    def index_of(positions):
        index = jnp.where(positions > ends[0], 1, 0)
        for end in ends[1:]:
            index = index + jnp.where(positions > end, 1, 0)
        return index

    at_end = jnp.where(
        (iota(square, 0) // heads) * LANES + iota(square, 1) == ends[0], running, 0.0
    )
    for h in range(heads):
        head_rows = (iota(square, 0) & (heads - 1)) == h
        first = jnp.sum(jnp.where(head_rows, at_end, 0.0), keepdims=True)
        first_ref[h : h + 1, :] = jnp.exp(jnp.broadcast_to(first, (1, LANES)))

    state[...] = jnp.zeros_like(state)
    ends_ref[...] = jnp.zeros_like(ends_ref)
    block = (CHUNK, CHUNK)
    per = CHUNK // LANES

    def chunk(c, carry):
        base = pl.multiple_of(c * CHUNK, CHUNK)
        span = pl.ds(base, CHUNK)
        index_col = index_of(base + iota((CHUNK, 1), 0))
        index_row = index_of(base + iota((1, CHUNK), 1))
        entry = index_of(base - 1)
        last = index_of(base + CHUNK - 1)
        linked = (index_col == index_row) & (iota(block, 0) >= iota(block, 1))
        for h in range(heads):
            cols = slice(h * DK, (h + 1) * DK)
            col = run_col[span, h : h + 1]
            row = jnp.concatenate(
                [run_row[pl.ds((per * c + i) * heads + h, 1), :] for i in range(per)], axis=1
            )
            at_last = row[:, CHUNK - 1 :]
            prior = run_row[pl.ds(jnp.maximum(per * c - 1, 0) * heads + h, 1), :]
            at_entry = jnp.where(c > 0, prior[:, LANES - 1 :], 0.0)
            query = q_ref[span, cols]
            key = k_ref[span, cols]
            value = v_ref[span, cols]
            scores = lax.dot_general(
                query, key, (((1,), (1,)), ((), ())), preferred_element_type=F32
            )
            weights = (scores * jnp.exp(jnp.where(linked, col - row, NEG))).astype(BF16)
            inside = jnp.dot(weights, value, preferred_element_type=F32)
            held = state[h]
            reach = jnp.exp(jnp.where(index_col == entry, col - at_entry, NEG))
            through = query_state(query, halves(held, 1))
            out_ref[span, cols] = inside + through * reach
            from_start = jnp.exp(jnp.where(index_col == 0, col, NEG))
            reached_ref[span, cols] = (query.astype(F32) * from_start).astype(BF16)
            wide_key = key.astype(F32)
            for k in range(ENDS):

                @pl.when((ends[k] >= base) & (ends[k] < base + CHUNK))
                def _():
                    here = base + iota((1, CHUNK), 1) == ends[k]
                    at_end = jnp.sum(jnp.where(here, row, 0.0), axis=1, keepdims=True)
                    weight = jnp.exp(jnp.where(index_col == k, at_end - col, NEG))
                    keep = jnp.exp(jnp.where(entry == k, at_end - at_entry, NEG))
                    ends_ref[k, h] = keep * held + outer_sum(wide_key * weight, value)

            weight = jnp.exp(jnp.where(index_col == last, at_last - col, NEG))
            keep = jnp.exp(jnp.where(entry == last, at_last - at_entry, NEG))
            state[h] = keep * held + outer_sum(wide_key * weight, value)
        return carry

    lax.fori_loop(0, tok // CHUNK, chunk, 0)
    open_end = index_of(jnp.int32(tok - 1)) == ended
    for h in range(heads):
        tail_ref[h] = jnp.where(open_end, state[h], 0.0)


def grid_of(head_size):
    return (4, 4, 2) if head_size == 32 else (1, 1, head_size)


def ring_kernel(
    steps,
    sizes,
    out_ref,
    reached_ref,
    ends_in,
    tail_ref,
    table_ref,
    first_ref,
    gain_ref,
    attended_ref,
    final_ref,
    ends_ref,
    mixed,
    sums,
    got,
    came,
    sent,
    carried,
    send_sem,
    recv_sem,
    tail_sems,
    sum_send,
    sum_recv,
):
    ring, head_size = sizes
    nx, ny, nc = grid_of(head_size)
    tok, width = out_ref.shape
    heads = width // DV
    tiles = tok // LANES
    z = lax.axis_index("seq")
    lane_id = lax.axis_index("head")
    core = lax.rem(lane_id, nc)
    y = lax.rem(lane_id // nc, ny)
    x = lane_id // (nc * ny)
    ahead = (lax.rem(z + 1, ring), lane_id)
    behind = (lax.rem(z + ring - 1, ring), lane_id)
    towards = (ahead, behind)
    stages = [
        [(z, (x * ny + y) * nc + lax.rem(core + d, nc)) for d in range(1, nc)],
        [(z, (lax.rem(x + d, nx) * ny + y) * nc + core) for d in range(1, nx)],
        [(z, (x * ny + lax.rem(y + d, ny)) * nc + core) for d in range(1, ny)],
    ]
    peers = [ahead, behind] + [peer for stage in stages for peer in stage]
    barrier = pltpu.get_barrier_semaphore()
    for peer in peers:
        pl.semaphore_signal(barrier, inc=1, device_id=peer, device_id_type=MESH)
    pl.semaphore_wait(barrier, len(peers))

    def tail_copy(h):
        return pltpu.make_async_remote_copy(
            src_ref=tail_ref.at[h],
            dst_ref=carried.at[h],
            send_sem=tail_sems.at[0, h],
            recv_sem=tail_sems.at[1, h],
            device_id=ahead,
            device_id_type=MESH,
        )

    def belt_copy(way, t, h):
        return pltpu.make_async_remote_copy(
            src_ref=sent.at[way, t, h],
            dst_ref=came.at[way, t, h],
            send_sem=send_sem.at[way, t, h],
            recv_sem=recv_sem.at[way, t, h],
            device_id=towards[way],
            device_id_type=MESH,
        )

    def sum_copies(stage):
        base = sum(len(s) for s in stages[:stage])
        return [
            pltpu.make_async_remote_copy(
                src_ref=sums.at[stage],
                dst_ref=got.at[base + i],
                send_sem=sum_send.at[base + i],
                recv_sem=sum_recv.at[base + i],
                device_id=peer,
                device_id_type=MESH,
            )
            for i, peer in enumerate(stages[stage])
        ]

    for h in range(heads):
        tail_copy(h).start()
    for k in range(1, ENDS):
        ends_ref[k] = ends_in[k]
    for h in range(heads):
        tail_copy(h).wait_recv()
        ends_ref[0, h] = ends_in[0, h] + first_ref[h : h + 1, :] * carried[h]

    def table_row(kind, t, way):
        return table_ref[pl.ds((kind + t) * 8 + way, 1), :]

    for row in range(SLOTS):
        for h in range(heads):
            value = jnp.zeros((DK, DV), F32)
            for k in range(ENDS):
                value = jnp.where(
                    table_row(2 * LONGEST, k, 0) == float(row + 1), ends_ref[k, h], value
                )
            final_ref[row, h] = value

    def send_step(t, first):
        for h in range(heads):
            for way in range(2):
                if first:
                    value = ends_ref[0, h]
                else:
                    belt_copy(way, t - 1, h).wait_recv()
                    value = came[way, t - 1, h]
                board = table_row(0, t, way)
                for k in range(ENDS):
                    value = jnp.where(board == float(k + 1), ends_ref[k, h], value)
                sent[way, t, h] = value
                belt_copy(way, t, h).start()

    def take_step(t):
        for h in range(heads):
            for way in range(2):
                value = came[way, t, h]
                take = table_row(LONGEST, t, way)
                for row in range(SLOTS):
                    final_ref[row, h] = jnp.where(
                        take == float(row + 1), value, final_ref[row, h]
                    )

    def mix():
        carried_halves = [halves(carried[h], 1) for h in range(heads)]
        ones = jnp.ones((8, 2 * width), BF16)
        per = CHUNK // LANES

        def body(c, carry):
            span = pl.ds(pl.multiple_of(c * CHUNK, CHUNK), CHUNK)
            parts = []
            for h in range(heads):
                cols = slice(h * DV, (h + 1) * DV)
                value = out_ref[span, cols] + query_state(
                    reached_ref[span, cols], carried_halves[h]
                )
                mixed[span, cols] = value
                parts.append(value)
            whole = jnp.concatenate(parts, axis=1)
            row_sums = lax.dot_general(
                ones,
                halves(whole * whole, 1),
                (((1,), (1,)), ((), ())),
                preferred_element_type=F32,
            )
            for i in range(per):
                sums[0, pl.ds(c * per + i, 1), :] = row_sums[:1, i * LANES : (i + 1) * LANES]
            return carry

        lax.fori_loop(0, tok // CHUNK, body, 0)

    def start_sums(stage):
        for copy in sum_copies(stage):
            copy.start()

    def join_sums(stage):
        base = sum(len(s) for s in stages[:stage])
        value = sums[stage]
        for i, copy in enumerate(sum_copies(stage)):
            copy.wait()
            value = value + got[base + i]
        sums[stage + 1] = value

    def normalize():
        mean = sums[3] * (1.0 / (width * head_size))
        inverse = lax.rsqrt(mean + EPSILON)
        turned = jnp.concatenate(
            [inverse, jnp.zeros((LANES - tiles, LANES), F32)], axis=0
        ).T
        gain = gain_ref[...]
        for c in range(tiles):
            span = slice(c * LANES, (c + 1) * LANES)
            scaled = mixed[span, :] * turned[:, c : c + 1] * gain
            attended_ref[span, :] = scaled.astype(BF16)

    send_step(0, True)
    mix()
    start_sums(0)
    send_step(1, False)
    take_step(0)
    join_sums(0)
    start_sums(1)
    send_step(2, False)
    take_step(1)
    join_sums(1)
    start_sums(2)
    send_step(3, False)
    take_step(2)
    join_sums(2)
    normalize()

    def step(t, carry):
        send_step(t, False)
        take_step(t - 1)
        return carry

    lax.fori_loop(4, steps, step, 0)
    for h in range(heads):
        for way in range(2):
            belt_copy(way, steps - 1, h).wait_recv()
    take_step(steps - 1)

    def drain(t, carry):
        for h in range(heads):
            for way in range(2):
                belt_copy(way, t, h).wait_send()
        return carry

    lax.fori_loop(0, steps, drain, 0)
    for h in range(heads):
        tail_copy(h).wait_send()


def vmem(count):
    return [pl.BlockSpec(memory_space=pltpu.VMEM)] * count


def solution(mesh):
    ring = mesh.shape["seq"]
    head_size = mesh.shape["head"]
    nx, ny, nc = grid_of(head_size)
    hops = (nc - 1) + (nx - 1) + (ny - 1)

    def shards(queries, key_rows, value_rows, log_decay, norm_gain, lengths, decode_slot):
        tok, width = queries.shape
        heads = log_decay.shape[0]
        tiles = tok // LANES
        prompts = lengths.shape[0]
        table_rows = (2 * LONGEST + ENDS + 1) * 8
        shape = jax.ShapeDtypeStruct
        smem = pl.BlockSpec(memory_space=pltpu.SMEM)
        *local, branch = pl.pallas_call(
            functools.partial(local_kernel, ring),
            out_shape=(
                shape((tok, width), F32),
                shape((tok, width), BF16),
                shape((ENDS, heads, DK, DV), F32),
                shape((heads, DK, DV), F32),
                shape((table_rows, LANES), F32),
                shape((8, LANES), F32),
                shape((1,), jnp.int32),
            ),
            in_specs=[smem, smem] + vmem(4),
            out_specs=tuple(vmem(6)) + (smem,),
            scratch_shapes=[
                pltpu.VMEM((LANES, LANES), F32),
                pltpu.VMEM((tok, LANES), F32),
                pltpu.VMEM((heads, DK, DV), F32),
                pltpu.SMEM((prompts,), jnp.int32),
            ],
            compiler_params=pltpu.CompilerParams(vmem_limit_bytes=48 << 20),
            name="local",
        )(lengths, decode_slot, log_decay, queries, key_rows, value_rows)

        def exchange(index, steps):
            belt = (2, steps, heads)
            return pl.pallas_call(
                functools.partial(ring_kernel, steps, (ring, head_size)),
                out_shape=(
                    shape((tok, width), BF16),
                    shape((SLOTS, heads, DK, DV), F32),
                ),
                in_specs=vmem(7),
                out_specs=tuple(vmem(2)),
                scratch_shapes=[
                    pltpu.VMEM((ENDS, heads, DK, DV), F32),
                    pltpu.VMEM((tok, width), F32),
                    pltpu.VMEM((4, tiles, LANES), F32),
                    pltpu.VMEM((max(hops, 1), tiles, LANES), F32),
                    pltpu.VMEM(belt + (DK, DV), F32),
                    pltpu.VMEM(belt + (DK, DV), F32),
                    pltpu.VMEM((heads, DK, DV), F32),
                    pltpu.SemaphoreType.DMA(belt),
                    pltpu.SemaphoreType.DMA(belt),
                    pltpu.SemaphoreType.DMA((2, heads)),
                    pltpu.SemaphoreType.DMA((max(hops, 1),)),
                    pltpu.SemaphoreType.DMA((max(hops, 1),)),
                ],
                compiler_params=pltpu.CompilerParams(
                    vmem_limit_bytes=48 << 20, collective_id=index, has_side_effects=True
                ),
                name=f"ring{steps}",
            )

        return lax.switch(
            branch[0],
            [exchange(index, steps) for index, steps in enumerate(LENGTHS)],
            *local,
            norm_gain.reshape(1, width),
        )

    in_specs = (
        P("seq", "head"),
        P("seq", "head"),
        P("seq", "head"),
        P("head", "seq"),
        P("head"),
        P(),
        P(),
    )
    out_specs = (P("seq", "head"), P("seq", "head", None, None))
    return jax.shard_map(shards, mesh=mesh, in_specs=in_specs, out_specs=out_specs, check_vma=False)
```

```python
import functools

import jax
import jax.numpy as jnp
from jax import lax
from jax.experimental import pallas as pl
from jax.experimental.pallas import tpu as pltpu
from jax.sharding import PartitionSpec as P

DK = 128
DV = 128
CHUNK = 256
SLOTS = 3
ENDS = 5
LANES = 128
LONGEST = 32
LENGTHS = (9, 10, 11, 12, 13, 14, 16, LONGEST)
PIECES = 4
FAR = 1 << 20
NEG = -1e30
EPSILON = 1e-06
MESH = pl.DeviceIdType.MESH
F32 = jnp.float32
BF16 = jnp.bfloat16
SORT5 = ((0, 1), (3, 4), (2, 4), (2, 3), (1, 4), (0, 3), (0, 2), (1, 3), (1, 2))
PRECISE = lax.Precision.HIGHEST


def iota(shape, axis):
    return lax.broadcasted_iota(jnp.int32, shape, axis)


def halves(wide, axis):
    upper = wide.astype(BF16)
    lower = (wide - upper.astype(F32)).astype(BF16)
    return jnp.concatenate([upper, lower], axis=axis)


def outer_sum(scaled_keys, values):
    both = lax.dot_general(
        halves(scaled_keys, 1), values, (((0,), (0,)), ((), ())), preferred_element_type=F32
    )
    return both[:DK] + both[DK:]


def query_state(rows, state_halves):
    both = jnp.dot(rows, state_halves, preferred_element_type=F32)
    return both[:, :DV] + both[:, DV:]


def route(me, ring, tok, prompts, finish, slot_ref, plan):
    shape = (8, LANES)
    sub, lane = iota(shape, 0), iota(shape, 1)
    place = lane & (ring - 1)
    leftward = (sub & 1) == 1
    dev = jnp.where(leftward, (ring - place) & (ring - 1), place)
    candidate = (lane // ring) * 4 + (sub >> 1)
    start = dev * tok
    first = jnp.zeros(shape, jnp.int32)
    for p in range(prompts):
        first = first + jnp.where(finish[p] < start, 1, 0)
    items = [jnp.zeros(shape, jnp.int32)] * ENDS
    for p in range(prompts):
        slot = slot_ref[p]
        owner = (slot * 43) >> 7
        value = owner * 4 + (slot - owner * SLOTS) + 1
        here = (finish[p] >= start) & (finish[p] < start + tok)
        rank = jnp.where(here, p - first, -1)
        items = [jnp.where(rank == k, value, item) for k, item in enumerate(items)]
    keys, own = [], []
    half = ring // 2
    for k, item in enumerate(items):
        owner, row = (item - 1) >> 2, (item - 1) & 3
        right = (owner - dev) & (ring - 1)
        left = (ring - right) & (ring - 1)
        mixed_bits = ((item * 37 + candidate * 1013 + 7) * 40503) >> 9
        draw = (mixed_bits ^ (mixed_bits >> 5)) & 7
        free = draw < jnp.where(right == half - 1, 6, jnp.where(right == half, 4, 2))
        fixed = (right < half) | ((right == half) & ((item & 1) == 0))
        near = (right >= half - 1) & (right <= half + 1) & (candidate > 0)
        go_right = (near & free) | (jnp.logical_not(near) & fixed)
        turned = (go_right & jnp.logical_not(leftward)) | (jnp.logical_not(go_right) & leftward)
        chosen = (item > 0) & (right > 0) & turned
        distance = jnp.where(leftward, left, right)
        keys.append(jnp.where(chosen, distance * 64 + k * 8 + row, 0))
        own.append(jnp.where((item > 0) & (right == 0), row + 1, 0))
    for a, b in SORT5:
        keys[a], keys[b] = jnp.maximum(keys[a], keys[b]), jnp.minimum(keys[a], keys[b])

    def turn(value, shift):
        wrapped = pltpu.roll(value, LANES - ring + shift, 1)
        return jnp.where(place < shift, wrapped, pltpu.roll(value, shift, 1))

    zero = jnp.zeros(shape, jnp.int32)
    belt, last = zero, zero
    for t in range(LONGEST):
        if t == 0:
            second = ((keys[0] >> 3) & 7) == 0
            riding = jnp.where(second, keys[1], keys[0])
            board = leftward & (riding > 0)
            following = [jnp.where(second, keys[0], keys[1])] + keys[2:] + [zero]
        else:
            riding = keys[0]
            board = (belt == 0) & (riding > 0)
            following = keys[1:] + [zero]
        boarded = jnp.where(board, ((riding >> 3) & 7) + 1, 0)
        belt = jnp.where(board, riding, belt)
        keys = [jnp.where(board, new, old) for new, old in zip(following, keys)]
        last = jnp.where(belt > 0, t + 1, last)
        moved = jnp.where(belt >= 128, belt - 64, jnp.where(belt >= 64, (belt & 7) + 1, 0))
        moved = turn(moved, 1)
        taken = jnp.where(moved < 64, moved, 0)
        belt = jnp.where(moved >= 64, moved, 0)
        plan[t] = boarded * 4 + taken
    shift = 1
    while shift < ring:
        last = jnp.maximum(last, turn(last, shift))
        shift *= 2
    other = jnp.where(leftward, pltpu.roll(last, 1, 0), pltpu.roll(last, 7, 0))
    best = jnp.min(jnp.maximum(last, other) * 32 + candidate)
    mirror = jnp.where(leftward, (ring - me) & (ring - 1), me)
    mine = (candidate == (best & 31)) & (place == mirror)
    tiles = [jnp.where(mine, plan[t], 0) for t in range(LONGEST)]
    tiles += [jnp.where(mine & jnp.logical_not(leftward), item, 0) for item in own]
    tiles += [zero] * (-len(tiles) % 16)
    stacked = jnp.concatenate(tiles, axis=0).astype(F32).astype(BF16)
    rows = stacked.shape[0]
    wide = jnp.dot(stacked, jnp.ones((LANES, LANES), BF16), preferred_element_type=F32)
    r0, r1 = iota((rows, rows), 0), iota((rows, rows), 1)
    gather = (((r0 ^ r1) & ~7) == 0) & (((r0 ^ r1) & 1) == 0)
    table = jnp.dot(
        gather.astype(F32).astype(BF16), wide.astype(BF16), preferred_element_type=F32
    )
    return table, best >> 5


def table_rows():
    return (-(-(LONGEST + ENDS) // 16) * 16) * 8


def index_of(positions, ends):
    index = jnp.where(positions > ends[0], 1, 0)
    for end in ends[1:]:
        index = index + jnp.where(positions > end, 1, 0)
    return index


def decay_parts(run_row, run_col, c, h, heads):
    per = CHUNK // LANES
    base = pl.multiple_of(c * CHUNK, CHUNK)
    col = run_col[pl.ds(base, CHUNK), h : h + 1]
    row = jnp.concatenate(
        [run_row[pl.ds((per * c + i) * heads + h, 1), :] for i in range(per)], axis=1
    )
    prior = run_row[pl.ds(jnp.maximum(per * c - 1, 0) * heads + h, 1), :]
    at_entry = jnp.where(c > 0, prior[:, LANES - 1 :], 0.0)
    return col, row, at_entry


def local_kernel(
    ring,
    len_hbm,
    slot_hbm,
    decay_hbm,
    k_hbm,
    v_hbm,
    held_ref,
    ends_ref,
    tail_ref,
    table_ref,
    first_ref,
    run_row,
    run_col,
    ends_out,
    branch_ref,
    len_ref,
    slot_ref,
    decay_ref,
    k_ref,
    v_ref,
    state,
    plan,
    finish_s,
    sems,
):
    tok = k_ref.shape[0]
    heads = decay_ref.shape[0]
    prompts = len_ref.shape[0]
    tiles = tok // LANES
    copies = [
        pltpu.make_async_copy(src, dst, sems.at[i])
        for i, (src, dst) in enumerate(
            [
                (len_hbm, len_ref),
                (slot_hbm, slot_ref),
                (decay_hbm, decay_ref),
                (k_hbm, k_ref),
                (v_hbm, v_ref),
            ]
        )
    ]
    for copy in copies:
        copy.start()
    me = lax.axis_index("seq")
    anchor = me * tok
    square = (LANES, LANES)
    copies[0].wait()
    copies[1].wait()
    copies[2].wait()

    decay = decay_ref[...]
    rows = jnp.concatenate(
        [decay[:, c * LANES : (c + 1) * LANES] for c in range(tiles)], axis=0
    )
    upper = (iota(square, 0) <= iota(square, 1)).astype(F32)
    within = jnp.dot(rows, upper, precision=PRECISE, preferred_element_type=F32)
    count = tiles * heads
    wide = jnp.concatenate([within, jnp.zeros((LANES - count, LANES), F32)], axis=0)
    totals = jnp.broadcast_to(wide[:, LANES - 1 :], square)
    earlier = (iota(square, 1) < iota(square, 0)) & (
        ((iota(square, 0) - iota(square, 1)) & (heads - 1)) == 0
    )
    running = wide + jnp.dot(
        earlier.astype(F32), totals, precision=PRECISE, preferred_element_type=F32
    )
    run_row[...] = running
    turned = running.T
    for c in range(tiles):
        shift = (LANES - heads * c) % LANES
        run_col[c * LANES : (c + 1) * LANES, :] = (
            pltpu.roll(turned, shift, 1) if shift else turned
        )

    total = jnp.int32(0)
    before = jnp.int32(0)
    ended = jnp.int32(0)
    finish = []
    for p in range(prompts):
        total = total + len_ref[p]
        finish.append(total - 1)
        finish_s[p] = total - 1
        before = before + jnp.where(total - 1 < anchor, 1, 0)
        ended = ended + jnp.where(total - 1 < anchor + tok, 1, 0)
    ended = ended - before
    ends = []
    for k in range(ENDS):
        place = finish_s[jnp.minimum(before + k, prompts - 1)] - anchor
        ends.append(jnp.where(k < ended, place, FAR))
        ends_out[k] = ends[k]

    table, steps = route(me, ring, tok, prompts, finish, slot_ref, plan)
    boards = jnp.floor(table * 0.25)
    table_ref[0] = boards
    table_ref[1] = table - 4.0 * boards
    branch = jnp.int32(0)
    for length in LENGTHS[:-1]:
        branch = branch + jnp.where(steps > length, 1, 0)
    branch_ref[0] = branch

    at_end = jnp.where(
        (iota(square, 0) // heads) * LANES + iota(square, 1) == ends[0], running, 0.0
    )
    for h in range(heads):
        head_rows = (iota(square, 0) & (heads - 1)) == h
        first = jnp.sum(jnp.where(head_rows, at_end, 0.0), keepdims=True)
        first_ref[h : h + 1, :] = jnp.exp(jnp.broadcast_to(first, (1, LANES)))

    copies[3].wait()
    copies[4].wait()
    ends_ref[...] = jnp.zeros_like(ends_ref)

    def chunk(c, held):
        base = pl.multiple_of(c * CHUNK, CHUNK)
        span = pl.ds(base, CHUNK)
        index_col = index_of(base + iota((CHUNK, 1), 0), ends)
        entry = index_of(base - 1, ends)
        last = index_of(base + CHUNK - 1, ends)
        following = []
        for h in range(heads):
            cols = slice(h * DK, (h + 1) * DK)
            col, row, at_entry = decay_parts(run_row, run_col, c, h, heads)
            at_last = row[:, CHUNK - 1 :]
            state[c, h] = held[h]
            held_ref[c, h] = halves(held[h], 1)
            weight = jnp.exp(jnp.where(index_col == last, at_last - col, NEG))
            keep = jnp.exp(jnp.where(entry == last, at_last - at_entry, NEG))
            fresh = outer_sum(k_ref[span, cols].astype(F32) * weight, v_ref[span, cols])
            following.append(keep * held[h] + fresh)
        return tuple(following)

    empty = tuple(jnp.zeros((DK, DV), F32) for _ in range(heads))
    held = lax.fori_loop(0, tok // CHUNK, chunk, empty)
    open_end = index_of(jnp.int32(tok - 1), ends) == ended
    for h in range(heads):
        tail_ref[h] = jnp.where(open_end, held[h], 0.0)

    def one_end(k, carry):
        place = finish_s[before + k] - anchor
        c = place // CHUNK
        base = pl.multiple_of(c * CHUNK, CHUNK)
        span = pl.ds(base, CHUNK)
        index_col = index_of(base + iota((CHUNK, 1), 0), ends)
        entry = index_of(base - 1, ends)
        here = base + iota((1, CHUNK), 1) == place
        for h in range(heads):
            cols = slice(h * DK, (h + 1) * DK)
            col, row, at_entry = decay_parts(run_row, run_col, c, h, heads)
            at_end = jnp.sum(jnp.where(here, row, 0.0), axis=1, keepdims=True)
            weight = jnp.exp(jnp.where(index_col == k, at_end - col, NEG))
            keep = jnp.exp(jnp.where(entry == k, at_end - at_entry, NEG))
            fresh = outer_sum(k_ref[span, cols].astype(F32) * weight, v_ref[span, cols])
            ends_ref[k, h] = keep * state[c, h] + fresh
        return carry

    lax.fori_loop(0, ended, one_end, 0)


def grid_of(head_size):
    return (4, 4, 2) if head_size == 32 else (1, 1, head_size)


def ring_kernel(
    steps,
    sizes,
    ends_s,
    q_hbm,
    k_hbm,
    v_hbm,
    held_ref,
    ends_in,
    tail_ref,
    table_ref,
    first_ref,
    run_row,
    run_col,
    gain_ref,
    attended_ref,
    final_ref,
    q_ref,
    k_ref,
    v_ref,
    ends_ref,
    mixed,
    sums,
    got,
    came,
    sent,
    load_sems,
    send_sem,
    recv_sem,
    sum_send,
    sum_recv,
):
    ring, head_size = sizes
    nx, ny, nc = grid_of(head_size)
    tok, width = q_ref.shape
    heads = width // DV
    tiles = tok // LANES
    piece = DK // PIECES
    loads = [
        pltpu.make_async_copy(src, dst, load_sems.at[i])
        for i, (src, dst) in enumerate([(q_hbm, q_ref), (k_hbm, k_ref), (v_hbm, v_ref)])
    ]
    for load in loads:
        load.start()
    z = lax.axis_index("seq")
    lane_id = lax.axis_index("head")
    core = lax.rem(lane_id, nc)
    y = lax.rem(lane_id // nc, ny)
    x = lane_id // (nc * ny)
    ahead = (lax.rem(z + 1, ring), lane_id)
    behind = (lax.rem(z + ring - 1, ring), lane_id)
    towards = (ahead, behind)
    stages = [
        [(z, (x * ny + y) * nc + lax.rem(core + d, nc)) for d in range(1, nc)],
        [(z, (lax.rem(x + d, nx) * ny + y) * nc + core) for d in range(1, nx)],
        [(z, (x * ny + lax.rem(y + d, ny)) * nc + core) for d in range(1, ny)],
    ]
    peers = [ahead, behind] + [peer for stage in stages for peer in stage]
    barrier = pltpu.get_barrier_semaphore()
    for peer in peers:
        pl.semaphore_signal(barrier, inc=1, device_id=peer, device_id_type=MESH)
    pl.semaphore_wait(barrier, len(peers))

    parts = [(h, i, slice(i * piece, (i + 1) * piece)) for h in range(heads) for i in range(PIECES)]

    def belt_copy(way, t, h, i, source=None):
        rows = slice(i * piece, (i + 1) * piece)
        return pltpu.make_async_remote_copy(
            src_ref=sent.at[way, t, h, rows] if source is None else source.at[h, rows],
            dst_ref=came.at[way, t, h, rows],
            send_sem=send_sem.at[way, t, h, i],
            recv_sem=recv_sem.at[way, t, h, i],
            device_id=towards[way],
            device_id_type=MESH,
        )

    def sum_copies(stage):
        base = sum(len(s) for s in stages[:stage])
        return [
            pltpu.make_async_remote_copy(
                src_ref=sums.at[stage],
                dst_ref=got.at[base + i],
                send_sem=sum_send.at[base + i],
                recv_sem=sum_recv.at[base + i],
                device_id=peer,
                device_id_type=MESH,
            )
            for i, peer in enumerate(stages[stage])
        ]

    def board_row(t, way):
        return table_ref[0, pl.ds(t * 8 + way, 1), :]

    def take_row(t, way):
        return table_ref[1, pl.ds(t * 8 + way, 1), :]

    def send_piece(way, t, part, value, source, lowest):
        h, i, rows = part
        board = board_row(t, way)
        for k in range(lowest, ENDS):
            value = jnp.where(board == float(k + 1), source[k, h, rows], value)
        sent[way, t, h, rows] = value
        belt_copy(way, t, h, i).start()

    def take_piece(way, t, part):
        h, i, rows = part
        value = came[way, t, h, rows]
        take = take_row(t, way)
        for row in range(SLOTS):
            final_ref[row, h, rows] = jnp.where(
                take == float(row + 1), value, final_ref[row, h, rows]
            )

    for h, i, rows in parts:
        belt_copy(0, 0, h, i, tail_ref).start()
    for part in parts:
        send_piece(1, 0, part, ends_in[0, part[0], part[2]], ends_in, 1)
    for k in range(1, ENDS):
        ends_ref[k] = ends_in[k]
    for load in loads:
        load.wait()
    for h, i, rows in parts:
        belt_copy(0, 0, h, i, tail_ref).wait_recv()
        ends_ref[0, h, rows] = ends_in[0, h, rows] + first_ref[h : h + 1, :] * came[0, 0, h, rows]
    for row in range(SLOTS):
        for h in range(heads):
            value = jnp.zeros((DK, DV), F32)
            for k in range(ENDS):
                kept = table_ref[1, (LONGEST + k) * 8 : (LONGEST + k) * 8 + 1, :]
                value = jnp.where(kept == float(row + 1), ends_ref[k, h], value)
            final_ref[row, h] = value

    ends = [ends_s[k] for k in range(ENDS)]
    block = (CHUNK, CHUNK)

    def attend(c):
        base = pl.multiple_of(c * CHUNK, CHUNK)
        span = pl.ds(base, CHUNK)
        index_col = index_of(base + iota((CHUNK, 1), 0), ends)
        index_row = index_of(base + iota((1, CHUNK), 1), ends)
        entry = index_of(base - 1, ends)
        linked = (index_col == index_row) & (iota(block, 0) >= iota(block, 1))
        for h in range(heads):
            cols = slice(h * DK, (h + 1) * DK)
            col, row, at_entry = decay_parts(run_row, run_col, c, h, heads)
            query = q_ref[span, cols]
            scores = lax.dot_general(
                query, k_ref[span, cols], (((1,), (1,)), ((), ())), preferred_element_type=F32
            )
            weights = (scores * jnp.exp(jnp.where(linked, col - row, NEG))).astype(BF16)
            inside = jnp.dot(weights, v_ref[span, cols], preferred_element_type=F32)
            reach = jnp.exp(jnp.where(index_col == entry, col - at_entry, NEG))
            through = query_state(query, held_ref[c, h])
            from_start = jnp.exp(jnp.where(index_col == 0, col, NEG))
            carried = query_state(query, halves(came[0, 0, h], 1))
            mixed[span, cols] = inside + through * reach + carried * from_start

    def square_sums(c, carry):
        per = CHUNK // LANES
        span = pl.ds(pl.multiple_of(c * CHUNK, CHUNK), CHUNK)
        whole = mixed[span, :]
        row_sums = lax.dot_general(
            jnp.ones((8, 2 * width), BF16),
            halves(whole * whole, 1),
            (((1,), (1,)), ((), ())),
            preferred_element_type=F32,
        )
        for i in range(per):
            sums[0, pl.ds(c * per + i, 1), :] = row_sums[:1, i * LANES : (i + 1) * LANES]
        return carry

    def start_sums(stage):
        for copy in sum_copies(stage):
            copy.start()

    def join_sums(stage):
        base = sum(len(s) for s in stages[:stage])
        value = sums[stage]
        for i, copy in enumerate(sum_copies(stage)):
            copy.wait()
            value = value + got[base + i]
        sums[stage + 1] = value

    def normalize():
        mean = sums[3] * (1.0 / (width * head_size))
        inverse = lax.rsqrt(mean + EPSILON)
        turned = jnp.concatenate(
            [inverse, jnp.zeros((LANES - tiles, LANES), F32)], axis=0
        ).T
        gain = gain_ref[...]
        for c in range(tiles):
            span = slice(c * LANES, (c + 1) * LANES)
            scaled = mixed[span, :] * turned[:, c : c + 1] * gain
            attended_ref[span, :] = scaled.astype(BF16)

    chunks = tok // CHUNK
    each = chunks // 4

    def step(t, carry):
        for part in parts:
            h, i, rows = part
            for way in range(2):
                if way == 0:

                    @pl.when(t > 1)
                    def _():
                        belt_copy(0, t - 1, h, i).wait_recv()
                else:
                    belt_copy(1, t - 1, h, i).wait_recv()
                send_piece(way, t, part, came[way, t - 1, h, rows], ends_ref, 0)
        for part in parts:
            for way in range(2):
                take_piece(way, t - 1, part)

        @pl.when(t <= 4)
        def _():
            def some(j, inner):
                attend((t - 1) * each + j)
                return inner

            lax.fori_loop(0, each, some, 0)

        @pl.when(t == 5)
        def _():
            lax.fori_loop(0, chunks, square_sums, 0)
            start_sums(0)

        @pl.when(t == 6)
        def _():
            join_sums(0)
            start_sums(1)

        @pl.when(t == 7)
        def _():
            join_sums(1)
            start_sums(2)

        @pl.when(t == 8)
        def _():
            join_sums(2)
            normalize()

        return carry

    lax.fori_loop(1, steps, step, 0)
    for part in parts:
        h, i, rows = part
        for way in range(2):
            belt_copy(way, steps - 1, h, i).wait_recv()
            take_piece(way, steps - 1, part)

    def drain(t, carry):
        for h, i, rows in parts:
            for way in range(2):
                belt_copy(way, t, h, i).wait_send()
        return carry

    lax.fori_loop(0, steps, drain, 0)


def store_kernel(attended, final, attended_hbm, final_hbm, sems):
    first = pltpu.make_async_copy(attended, attended_hbm, sems.at[0])
    second = pltpu.make_async_copy(final, final_hbm, sems.at[1])
    first.start()
    second.start()
    first.wait()
    second.wait()


def vmem(count):
    return [pl.BlockSpec(memory_space=pltpu.VMEM)] * count


def hbm(count):
    return [pl.BlockSpec(memory_space=pltpu.HBM)] * count


def solution(mesh):
    ring = mesh.shape["seq"]
    head_size = mesh.shape["head"]
    nx, ny, nc = grid_of(head_size)
    hops = (nc - 1) + (nx - 1) + (ny - 1)

    def shards(queries, key_rows, value_rows, log_decay, norm_gain, lengths, decode_slot):
        tok, width = queries.shape
        heads = log_decay.shape[0]
        tiles = tok // LANES
        prompts = lengths.shape[0]
        shape = jax.ShapeDtypeStruct
        smem = pl.BlockSpec(memory_space=pltpu.SMEM)
        chunks = tok // CHUNK
        *local, ends, branch = pl.pallas_call(
            functools.partial(local_kernel, ring),
            out_shape=(
                shape((chunks, heads, DK, 2 * DV), BF16),
                shape((ENDS, heads, DK, DV), F32),
                shape((heads, DK, DV), F32),
                shape((2, table_rows(), LANES), F32),
                shape((8, LANES), F32),
                shape((LANES, LANES), F32),
                shape((tok, LANES), F32),
                shape((ENDS,), jnp.int32),
                shape((1,), jnp.int32),
            ),
            in_specs=hbm(5),
            out_specs=tuple(vmem(7)) + (smem, smem),
            scratch_shapes=[
                pltpu.SMEM((prompts,), jnp.int32),
                pltpu.SMEM((prompts,), jnp.int32),
                pltpu.VMEM((heads, tok), F32),
                pltpu.VMEM((tok, width), BF16),
                pltpu.VMEM((tok, width), BF16),
                pltpu.VMEM((chunks, heads, DK, DV), F32),
                pltpu.VMEM((LONGEST, 8, LANES), jnp.int32),
                pltpu.SMEM((prompts,), jnp.int32),
                pltpu.SemaphoreType.DMA((5,)),
            ],
            compiler_params=pltpu.CompilerParams(vmem_limit_bytes=40 << 20),
            name="local",
        )(lengths, decode_slot, log_decay, key_rows, value_rows)

        outs = (shape((tok, width), BF16), shape((SLOTS, heads, DK, DV), F32))

        def exchange(index, steps):
            belt = (2, steps, heads)
            ring_call = pl.pallas_call(
                functools.partial(ring_kernel, steps, (ring, head_size)),
                out_shape=outs,
                in_specs=[smem] + hbm(3) + vmem(8),
                out_specs=tuple(vmem(2)),
                scratch_shapes=[
                    pltpu.VMEM((tok, width), BF16),
                    pltpu.VMEM((tok, width), BF16),
                    pltpu.VMEM((tok, width), BF16),
                    pltpu.VMEM((ENDS, heads, DK, DV), F32),
                    pltpu.VMEM((tok, width), F32),
                    pltpu.VMEM((4, tiles, LANES), F32),
                    pltpu.VMEM((max(hops, 1), tiles, LANES), F32),
                    pltpu.VMEM(belt + (DK, DV), F32),
                    pltpu.VMEM(belt + (DK, DV), F32),
                    pltpu.SemaphoreType.DMA((3,)),
                    pltpu.SemaphoreType.DMA(belt + (PIECES,)),
                    pltpu.SemaphoreType.DMA(belt + (PIECES,)),
                    pltpu.SemaphoreType.DMA((max(hops, 1),)),
                    pltpu.SemaphoreType.DMA((max(hops, 1),)),
                ],
                compiler_params=pltpu.CompilerParams(
                    vmem_limit_bytes=48 << 20, collective_id=index, has_side_effects=True
                ),
                name=f"ring{steps}",
            )
            store_call = pl.pallas_call(
                store_kernel,
                out_shape=outs,
                in_specs=vmem(2),
                out_specs=tuple(hbm(2)),
                scratch_shapes=[pltpu.SemaphoreType.DMA((2,))],
                compiler_params=pltpu.CompilerParams(vmem_limit_bytes=4 << 20),
                name="store",
            )
            return lambda *operands: store_call(*ring_call(*operands))

        return lax.switch(
            branch[0],
            [exchange(index, steps) for index, steps in enumerate(LENGTHS)],
            ends,
            queries,
            key_rows,
            value_rows,
            *local,
            norm_gain.reshape(1, width),
        )

    in_specs = (
        P("seq", "head"),
        P("seq", "head"),
        P("seq", "head"),
        P("head", "seq"),
        P("head"),
        P(),
        P(),
    )
    out_specs = (P("seq", "head"), P("seq", "head", None, None))
    return jax.shard_map(shards, mesh=mesh, in_specs=in_specs, out_specs=out_specs, check_vma=False)
```

```python
import functools

import jax
import jax.numpy as jnp
from jax import lax
from jax.experimental import pallas as pl
from jax.experimental.pallas import tpu as pltpu
from jax.sharding import PartitionSpec as P

DK = 128
DV = 128
CHUNK = 256
SLOTS = 3
ENDS = 5
LANES = 128
LONGEST = 32
LENGTHS = (9, 10, 11, 12, 13, 14, 16, LONGEST)
PIECES = 2
FAR = 1 << 20
NEG = -1e30
EPSILON = 1e-06
MESH = pl.DeviceIdType.MESH
F32 = jnp.float32
BF16 = jnp.bfloat16
SORT5 = ((0, 1), (3, 4), (2, 4), (2, 3), (1, 4), (0, 3), (0, 2), (1, 3), (1, 2))
PRECISE = lax.Precision.HIGHEST


def iota(shape, axis):
    return lax.broadcasted_iota(jnp.int32, shape, axis)


def halves(wide, axis):
    upper = wide.astype(BF16)
    lower = (wide - upper.astype(F32)).astype(BF16)
    return jnp.concatenate([upper, lower], axis=axis)


def outer_sum(turned_keys, weight_row, values):
    scaled = halves(turned_keys.astype(F32) * weight_row, 0)
    both = jnp.dot(scaled, values, preferred_element_type=F32)
    return both[:DK] + both[DK:]


def query_state(rows, state_halves):
    both = jnp.dot(rows, state_halves, preferred_element_type=F32)
    return both[:, :DV] + both[:, DV:]


def route(me, ring, tok, prompts, finish, slot_ref, plan):
    shape = (8, LANES)
    sub, lane = iota(shape, 0), iota(shape, 1)
    place = lane & (ring - 1)
    leftward = (sub & 1) == 1
    dev = jnp.where(leftward, (ring - place) & (ring - 1), place)
    candidate = (lane // ring) * 4 + (sub >> 1)
    start = dev * tok
    first = jnp.zeros(shape, jnp.int32)
    for p in range(prompts):
        first = first + jnp.where(finish[p] < start, 1, 0)
    items = [jnp.zeros(shape, jnp.int32)] * ENDS
    for p in range(prompts):
        slot = slot_ref[p]
        owner = (slot * 43) >> 7
        value = owner * 4 + (slot - owner * SLOTS) + 1
        here = (finish[p] >= start) & (finish[p] < start + tok)
        rank = jnp.where(here, p - first, -1)
        items = [jnp.where(rank == k, value, item) for k, item in enumerate(items)]
    keys, own = [], []
    half = ring // 2
    for k, item in enumerate(items):
        owner, row = (item - 1) >> 2, (item - 1) & 3
        right = (owner - dev) & (ring - 1)
        left = (ring - right) & (ring - 1)
        mixed_bits = item * (2 * candidate + 1) * 40503 + candidate * 7919
        draw = ((mixed_bits >> 11) ^ (mixed_bits >> 6)) & 31
        free = draw < 16 + (half - right) * 5
        fixed = (right < half) | ((right == half) & ((item & 1) == 0))
        near = (right >= half - 3) & (right <= half + 3) & (candidate > 0)
        go_right = (near & free) | (jnp.logical_not(near) & fixed)
        turned = (go_right & jnp.logical_not(leftward)) | (jnp.logical_not(go_right) & leftward)
        chosen = (item > 0) & (right > 0) & turned
        distance = jnp.where(leftward, left, right)
        keys.append(jnp.where(chosen, distance * 64 + k * 8 + row, 0))
        own.append(jnp.where((item > 0) & (right == 0), row + 1, 0))
    for a, b in SORT5:
        keys[a], keys[b] = jnp.maximum(keys[a], keys[b]), jnp.minimum(keys[a], keys[b])

    def turn(value, shift):
        wrapped = pltpu.roll(value, LANES - ring + shift, 1)
        return jnp.where(place < shift, wrapped, pltpu.roll(value, shift, 1))

    zero = jnp.zeros(shape, jnp.int32)
    belt, last = zero, zero
    for t in range(LONGEST):
        if t == 0:
            second = ((keys[0] >> 3) & 7) == 0
            riding = jnp.where(second, keys[1], keys[0])
            board = leftward & (riding > 0)
            following = [jnp.where(second, keys[0], keys[1])] + keys[2:] + [zero]
        else:
            riding = keys[0]
            board = (belt == 0) & (riding > 0)
            following = keys[1:] + [zero]
        boarded = jnp.where(board, ((riding >> 3) & 7) + 1, 0)
        belt = jnp.where(board, riding, belt)
        keys = [jnp.where(board, new, old) for new, old in zip(following, keys)]
        last = jnp.where(belt > 0, t + 1, last)
        moved = jnp.where(belt >= 128, belt - 64, jnp.where(belt >= 64, (belt & 7) + 1, 0))
        moved = turn(moved, 1)
        taken = jnp.where(moved < 64, moved, 0)
        belt = jnp.where(moved >= 64, moved, 0)
        plan[t] = boarded * 4 + taken
    shift = 1
    while shift < ring:
        last = jnp.maximum(last, turn(last, shift))
        shift *= 2
    other = jnp.where(leftward, pltpu.roll(last, 1, 0), pltpu.roll(last, 7, 0))
    best = jnp.min(jnp.maximum(last, other) * 32 + candidate)
    mirror = jnp.where(leftward, (ring - me) & (ring - 1), me)
    mine = (candidate == (best & 31)) & (place == mirror)
    tiles = [jnp.where(mine, plan[t], 0) for t in range(LONGEST)]
    tiles += [jnp.where(mine & jnp.logical_not(leftward), item, 0) for item in own]
    tiles += [zero] * (-len(tiles) % 16)
    stacked = jnp.concatenate(tiles, axis=0).astype(F32).astype(BF16)
    rows = stacked.shape[0]
    wide = jnp.dot(stacked, jnp.ones((LANES, LANES), BF16), preferred_element_type=F32)
    r0, r1 = iota((rows, rows), 0), iota((rows, rows), 1)
    gather = (((r0 ^ r1) & ~7) == 0) & (((r0 ^ r1) & 1) == 0)
    table = jnp.dot(
        gather.astype(F32).astype(BF16), wide.astype(BF16), preferred_element_type=F32
    )
    return table, best >> 5


def table_rows():
    return (-(-(LONGEST + ENDS) // 16) * 16) * 8


def index_of(positions, ends):
    index = jnp.where(positions > ends[0], 1, 0)
    for end in ends[1:]:
        index = index + jnp.where(positions > end, 1, 0)
    return index


def decay_row(run_row, c, h, heads):
    per = CHUNK // LANES
    row = jnp.concatenate(
        [run_row[pl.ds((per * c + i) * heads + h, 1), :] for i in range(per)], axis=1
    )
    prior = run_row[pl.ds(jnp.maximum(per * c - 1, 0) * heads + h, 1), :]
    at_entry = jnp.where(c > 0, prior[:, LANES - 1 :], 0.0)
    return row, at_entry


def local_kernel(
    ring,
    len_hbm,
    slot_hbm,
    decay_hbm,
    k_hbm,
    v_hbm,
    held_ref,
    ends_ref,
    tail_ref,
    table_ref,
    first_ref,
    run_row,
    ends_out,
    branch_ref,
    len_ref,
    slot_ref,
    decay_ref,
    k_ref,
    v_ref,
    state,
    keys_t,
    plan,
    finish_s,
    sems,
):
    tok = k_ref.shape[0]
    heads = decay_ref.shape[0]
    prompts = len_ref.shape[0]
    tiles = tok // LANES
    copies = [
        pltpu.make_async_copy(src, dst, sems.at[i])
        for i, (src, dst) in enumerate(
            [
                (len_hbm, len_ref),
                (slot_hbm, slot_ref),
                (decay_hbm, decay_ref),
                (k_hbm, k_ref),
                (v_hbm, v_ref),
            ]
        )
    ]
    for copy in copies:
        copy.start()
    me = lax.axis_index("seq")
    anchor = me * tok
    square = (LANES, LANES)
    copies[0].wait()
    copies[1].wait()
    copies[2].wait()

    decay = decay_ref[...]
    rows = jnp.concatenate(
        [decay[:, c * LANES : (c + 1) * LANES] for c in range(tiles)], axis=0
    )
    upper = (iota(square, 0) <= iota(square, 1)).astype(F32)
    within = jnp.dot(rows, upper, precision=PRECISE, preferred_element_type=F32)
    count = tiles * heads
    wide = jnp.concatenate([within, jnp.zeros((LANES - count, LANES), F32)], axis=0)
    totals = jnp.broadcast_to(wide[:, LANES - 1 :], square)
    earlier = (iota(square, 1) < iota(square, 0)) & (
        ((iota(square, 0) - iota(square, 1)) & (heads - 1)) == 0
    )
    running = wide + jnp.dot(
        earlier.astype(F32), totals, precision=PRECISE, preferred_element_type=F32
    )
    run_row[...] = running

    total = jnp.int32(0)
    before = jnp.int32(0)
    ended = jnp.int32(0)
    finish = []
    for p in range(prompts):
        total = total + len_ref[p]
        finish.append(total - 1)
        finish_s[p] = total - 1
        before = before + jnp.where(total - 1 < anchor, 1, 0)
        ended = ended + jnp.where(total - 1 < anchor + tok, 1, 0)
    ended = ended - before
    ends = []
    for k in range(ENDS):
        place = finish_s[jnp.minimum(before + k, prompts - 1)] - anchor
        ends.append(jnp.where(k < ended, place, FAR))
        ends_out[k] = ends[k]

    table, steps = route(me, ring, tok, prompts, finish, slot_ref, plan)
    boards = jnp.floor(table * 0.25)
    table_ref[0] = boards
    table_ref[1] = table - 4.0 * boards
    branch = jnp.int32(0)
    for length in LENGTHS[:-1]:
        branch = branch + jnp.where(steps > length, 1, 0)
    branch_ref[0] = branch

    at_end = jnp.where(
        (iota(square, 0) // heads) * LANES + iota(square, 1) == ends[0], running, 0.0
    )
    for h in range(heads):
        head_rows = (iota(square, 0) & (heads - 1)) == h
        first = jnp.sum(jnp.where(head_rows, at_end, 0.0), keepdims=True)
        first_ref[h : h + 1, :] = jnp.exp(jnp.broadcast_to(first, (1, LANES)))

    copies[3].wait()
    copies[4].wait()
    ends_ref[...] = jnp.zeros_like(ends_ref)

    def chunk(c, held):
        base = pl.multiple_of(c * CHUNK, CHUNK)
        span = pl.ds(base, CHUNK)
        index_row = index_of(base + iota((1, CHUNK), 1), ends)
        entry = index_of(base - 1, ends)
        last = index_of(base + CHUNK - 1, ends)
        following = []
        for h in range(heads):
            cols = slice(h * DK, (h + 1) * DK)
            row, at_entry = decay_row(run_row, c, h, heads)
            at_last = row[:, CHUNK - 1 :]
            state[c, h] = held[h]
            held_ref[c, h] = halves(held[h], 1)
            turned_keys = k_ref[span, cols].T
            keys_t[c, h] = turned_keys
            weight = jnp.exp(jnp.where(index_row == last, at_last - row, NEG))
            keep = jnp.exp(jnp.where(entry == last, at_last - at_entry, NEG))
            fresh = outer_sum(turned_keys, weight, v_ref[span, cols])
            following.append(keep * held[h] + fresh)
        return tuple(following)

    empty = tuple(jnp.zeros((DK, DV), F32) for _ in range(heads))
    held = lax.fori_loop(0, tok // CHUNK, chunk, empty, unroll=2)
    open_end = index_of(jnp.int32(tok - 1), ends) == ended
    for h in range(heads):
        tail_ref[h] = jnp.where(open_end, held[h], 0.0)

    def one_end(k, carry):
        place = finish_s[before + k] - anchor
        c = place // CHUNK
        base = pl.multiple_of(c * CHUNK, CHUNK)
        span = pl.ds(base, CHUNK)
        positions = base + iota((1, CHUNK), 1)
        index_row = index_of(positions, ends)
        entry = index_of(base - 1, ends)
        for h in range(heads):
            cols = slice(h * DK, (h + 1) * DK)
            row, at_entry = decay_row(run_row, c, h, heads)
            at_end = jnp.sum(jnp.where(positions == place, row, 0.0), axis=1, keepdims=True)
            weight = jnp.exp(jnp.where(index_row == k, at_end - row, NEG))
            keep = jnp.exp(jnp.where(entry == k, at_end - at_entry, NEG))
            fresh = outer_sum(keys_t[c, h], weight, v_ref[span, cols])
            ends_ref[k, h] = keep * state[c, h] + fresh
        return carry

    lax.fori_loop(0, ended, one_end, 0)


def grid_of(head_size):
    return (4, 4, 2) if head_size == 32 else (1, 1, head_size)


def ring_kernel(
    steps,
    sizes,
    ends_s,
    q_hbm,
    k_hbm,
    v_hbm,
    held_ref,
    ends_in,
    tail_ref,
    table_ref,
    first_ref,
    run_row,
    gain_ref,
    attended_ref,
    final_ref,
    q_ref,
    k_ref,
    v_ref,
    ends_ref,
    run_col,
    mixed,
    sums,
    got,
    came,
    sent,
    load_sems,
    send_sem,
    recv_sem,
    sum_send,
    sum_recv,
):
    ring, head_size = sizes
    nx, ny, nc = grid_of(head_size)
    tok, width = q_ref.shape
    heads = width // DV
    tiles = tok // LANES
    piece = DK // PIECES
    loads = [
        pltpu.make_async_copy(src, dst, load_sems.at[i])
        for i, (src, dst) in enumerate([(q_hbm, q_ref), (k_hbm, k_ref), (v_hbm, v_ref)])
    ]
    for load in loads:
        load.start()
    z = lax.axis_index("seq")
    lane_id = lax.axis_index("head")
    core = lax.rem(lane_id, nc)
    y = lax.rem(lane_id // nc, ny)
    x = lane_id // (nc * ny)
    ahead = (lax.rem(z + 1, ring), lane_id)
    behind = (lax.rem(z + ring - 1, ring), lane_id)
    towards = (ahead, behind)
    stages = [
        [(z, (x * ny + y) * nc + lax.rem(core + d, nc)) for d in range(1, nc)],
        [(z, (lax.rem(x + d, nx) * ny + y) * nc + core) for d in range(1, nx)],
        [(z, (x * ny + lax.rem(y + d, ny)) * nc + core) for d in range(1, ny)],
    ]
    peers = [ahead, behind] + [peer for stage in stages for peer in stage]
    barrier = pltpu.get_barrier_semaphore()
    for peer in peers:
        pl.semaphore_signal(barrier, inc=1, device_id=peer, device_id_type=MESH)
    pl.semaphore_wait(barrier, len(peers))

    parts = [(h, i, slice(i * piece, (i + 1) * piece)) for h in range(heads) for i in range(PIECES)]

    def belt_copy(way, t, h, i, source=None):
        rows = slice(i * piece, (i + 1) * piece)
        return pltpu.make_async_remote_copy(
            src_ref=sent.at[way, t, h, rows] if source is None else source.at[h, rows],
            dst_ref=came.at[way, t, h, rows],
            send_sem=send_sem.at[way, t, h, i],
            recv_sem=recv_sem.at[way, t, h, i],
            device_id=towards[way],
            device_id_type=MESH,
        )

    def sum_copies(stage):
        base = sum(len(s) for s in stages[:stage])
        return [
            pltpu.make_async_remote_copy(
                src_ref=sums.at[stage],
                dst_ref=got.at[base + i],
                send_sem=sum_send.at[base + i],
                recv_sem=sum_recv.at[base + i],
                device_id=peer,
                device_id_type=MESH,
            )
            for i, peer in enumerate(stages[stage])
        ]

    def board_row(t, way):
        return table_ref[0, pl.ds(t * 8 + way, 1), :]

    def take_row(t, way):
        return table_ref[1, pl.ds(t * 8 + way, 1), :]

    def send_piece(way, t, part, value, source, lowest):
        h, i, rows = part
        board = board_row(t, way)
        for k in range(lowest, ENDS):
            value = jnp.where(board == float(k + 1), source[k, h, rows], value)
        sent[way, t, h, rows] = value
        belt_copy(way, t, h, i).start()

    def take_piece(way, t, part):
        h, i, rows = part
        value = came[way, t, h, rows]
        take = take_row(t, way)
        for row in range(SLOTS):
            final_ref[row, h, rows] = jnp.where(
                take == float(row + 1), value, final_ref[row, h, rows]
            )

    for h, i, rows in parts:
        belt_copy(0, 0, h, i, tail_ref).start()
    for part in parts:
        send_piece(1, 0, part, ends_in[0, part[0], part[2]], ends_in, 1)
    for k in range(1, ENDS):
        ends_ref[k] = ends_in[k]
    turned = run_row[...].T
    for c in range(tiles):
        shift = (LANES - heads * c) % LANES
        run_col[c * LANES : (c + 1) * LANES, :] = (
            pltpu.roll(turned, shift, 1) if shift else turned
        )
    for load in loads:
        load.wait()
    for h, i, rows in parts:
        belt_copy(0, 0, h, i, tail_ref).wait_recv()
        ends_ref[0, h, rows] = ends_in[0, h, rows] + first_ref[h : h + 1, :] * came[0, 0, h, rows]
    for row in range(SLOTS):
        for h in range(heads):
            value = jnp.zeros((DK, DV), F32)
            for k in range(ENDS):
                kept = table_ref[1, (LONGEST + k) * 8 : (LONGEST + k) * 8 + 1, :]
                value = jnp.where(kept == float(row + 1), ends_ref[k, h], value)
            final_ref[row, h] = value

    ends = [ends_s[k] for k in range(ENDS)]
    block = (CHUNK, CHUNK)

    def attend(c):
        base = pl.multiple_of(c * CHUNK, CHUNK)
        span = pl.ds(base, CHUNK)
        index_col = index_of(base + iota((CHUNK, 1), 0), ends)
        index_row = index_of(base + iota((1, CHUNK), 1), ends)
        entry = index_of(base - 1, ends)
        linked = (index_col == index_row) & (iota(block, 0) >= iota(block, 1))
        for h in range(heads):
            cols = slice(h * DK, (h + 1) * DK)
            row, at_entry = decay_row(run_row, c, h, heads)
            col = run_col[span, h : h + 1]
            query = q_ref[span, cols]
            scores = lax.dot_general(
                query, k_ref[span, cols], (((1,), (1,)), ((), ())), preferred_element_type=F32
            )
            weights = (scores * jnp.exp(jnp.where(linked, col - row, NEG))).astype(BF16)
            inside = jnp.dot(weights, v_ref[span, cols], preferred_element_type=F32)
            reach = jnp.exp(jnp.where(index_col == entry, col - at_entry, NEG))
            through = query_state(query, held_ref[c, h])
            from_start = jnp.exp(jnp.where(index_col == 0, col, NEG))
            carried = query_state(query, halves(came[0, 0, h], 1))
            mixed[span, cols] = inside + through * reach + carried * from_start

    def square_sums(c, carry):
        per = CHUNK // LANES
        span = pl.ds(pl.multiple_of(c * CHUNK, CHUNK), CHUNK)
        whole = mixed[span, :]
        row_sums = lax.dot_general(
            jnp.ones((8, 2 * width), BF16),
            halves(whole * whole, 1),
            (((1,), (1,)), ((), ())),
            preferred_element_type=F32,
        )
        for i in range(per):
            sums[0, pl.ds(c * per + i, 1), :] = row_sums[:1, i * LANES : (i + 1) * LANES]
        return carry

    def start_sums(stage):
        for copy in sum_copies(stage):
            copy.start()

    def join_sums(stage):
        base = sum(len(s) for s in stages[:stage])
        value = sums[stage]
        for i, copy in enumerate(sum_copies(stage)):
            copy.wait()
            value = value + got[base + i]
        sums[stage + 1] = value

    def normalize():
        mean = sums[3] * (1.0 / (width * head_size))
        inverse = lax.rsqrt(mean + EPSILON)
        turned = jnp.concatenate(
            [inverse, jnp.zeros((LANES - tiles, LANES), F32)], axis=0
        ).T
        gain = gain_ref[...]
        for c in range(tiles):
            span = slice(c * LANES, (c + 1) * LANES)
            scaled = mixed[span, :] * turned[:, c : c + 1] * gain
            attended_ref[span, :] = scaled.astype(BF16)

    chunks = tok // CHUNK
    each = chunks // 4

    def step(t, carry):
        for part in parts:
            h, i, rows = part
            for way in range(2):
                if way == 0:

                    @pl.when(t > 1)
                    def _():
                        belt_copy(0, t - 1, h, i).wait_recv()
                else:
                    belt_copy(1, t - 1, h, i).wait_recv()
                send_piece(way, t, part, came[way, t - 1, h, rows], ends_ref, 0)
        for part in parts:
            for way in range(2):
                take_piece(way, t - 1, part)

        @pl.when(t <= 4)
        def _():
            def some(j, inner):
                attend((t - 1) * each + j)
                return inner

            lax.fori_loop(0, each, some, 0)

        @pl.when(t == 5)
        def _():
            lax.fori_loop(0, chunks, square_sums, 0)
            start_sums(0)

        @pl.when(t == 6)
        def _():
            join_sums(0)
            start_sums(1)

        @pl.when(t == 7)
        def _():
            join_sums(1)
            start_sums(2)

        @pl.when(t == 8)
        def _():
            join_sums(2)
            normalize()

        return carry

    lax.fori_loop(1, steps, step, 0)
    for part in parts:
        h, i, rows = part
        for way in range(2):
            belt_copy(way, steps - 1, h, i).wait_recv()
            take_piece(way, steps - 1, part)

    def drain(t, carry):
        for h, i, rows in parts:
            for way in range(2):
                belt_copy(way, t, h, i).wait_send()
        return carry

    lax.fori_loop(0, steps, drain, 0)


def store_kernel(attended, final, attended_hbm, final_hbm, sems):
    first = pltpu.make_async_copy(attended, attended_hbm, sems.at[0])
    second = pltpu.make_async_copy(final, final_hbm, sems.at[1])
    first.start()
    second.start()
    first.wait()
    second.wait()


def vmem(count):
    return [pl.BlockSpec(memory_space=pltpu.VMEM)] * count


def hbm(count):
    return [pl.BlockSpec(memory_space=pltpu.HBM)] * count


def solution(mesh):
    ring = mesh.shape["seq"]
    head_size = mesh.shape["head"]
    nx, ny, nc = grid_of(head_size)
    hops = (nc - 1) + (nx - 1) + (ny - 1)

    def shards(queries, key_rows, value_rows, log_decay, norm_gain, lengths, decode_slot):
        tok, width = queries.shape
        heads = log_decay.shape[0]
        tiles = tok // LANES
        prompts = lengths.shape[0]
        shape = jax.ShapeDtypeStruct
        smem = pl.BlockSpec(memory_space=pltpu.SMEM)
        chunks = tok // CHUNK
        *local, ends, branch = pl.pallas_call(
            functools.partial(local_kernel, ring),
            out_shape=(
                shape((chunks, heads, DK, 2 * DV), BF16),
                shape((ENDS, heads, DK, DV), F32),
                shape((heads, DK, DV), F32),
                shape((2, table_rows(), LANES), F32),
                shape((8, LANES), F32),
                shape((LANES, LANES), F32),
                shape((ENDS,), jnp.int32),
                shape((1,), jnp.int32),
            ),
            in_specs=hbm(5),
            out_specs=tuple(vmem(6)) + (smem, smem),
            scratch_shapes=[
                pltpu.SMEM((prompts,), jnp.int32),
                pltpu.SMEM((prompts,), jnp.int32),
                pltpu.VMEM((heads, tok), F32),
                pltpu.VMEM((tok, width), BF16),
                pltpu.VMEM((tok, width), BF16),
                pltpu.VMEM((chunks, heads, DK, DV), F32),
                pltpu.VMEM((chunks, heads, DK, CHUNK), BF16),
                pltpu.VMEM((LONGEST, 8, LANES), jnp.int32),
                pltpu.SMEM((prompts,), jnp.int32),
                pltpu.SemaphoreType.DMA((5,)),
            ],
            compiler_params=pltpu.CompilerParams(vmem_limit_bytes=40 << 20),
            name="local",
        )(lengths, decode_slot, log_decay, key_rows, value_rows)

        outs = (shape((tok, width), BF16), shape((SLOTS, heads, DK, DV), F32))

        def exchange(index, steps):
            belt = (2, steps, heads)
            ring_call = pl.pallas_call(
                functools.partial(ring_kernel, steps, (ring, head_size)),
                out_shape=outs,
                in_specs=[smem] + hbm(3) + vmem(7),
                out_specs=tuple(vmem(2)),
                scratch_shapes=[
                    pltpu.VMEM((tok, width), BF16),
                    pltpu.VMEM((tok, width), BF16),
                    pltpu.VMEM((tok, width), BF16),
                    pltpu.VMEM((ENDS, heads, DK, DV), F32),
                    pltpu.VMEM((tok, LANES), F32),
                    pltpu.VMEM((tok, width), F32),
                    pltpu.VMEM((4, tiles, LANES), F32),
                    pltpu.VMEM((max(hops, 1), tiles, LANES), F32),
                    pltpu.VMEM(belt + (DK, DV), F32),
                    pltpu.VMEM(belt + (DK, DV), F32),
                    pltpu.SemaphoreType.DMA((3,)),
                    pltpu.SemaphoreType.DMA(belt + (PIECES,)),
                    pltpu.SemaphoreType.DMA(belt + (PIECES,)),
                    pltpu.SemaphoreType.DMA((max(hops, 1),)),
                    pltpu.SemaphoreType.DMA((max(hops, 1),)),
                ],
                compiler_params=pltpu.CompilerParams(
                    vmem_limit_bytes=48 << 20, collective_id=index, has_side_effects=True
                ),
                name=f"ring{steps}",
            )
            store_call = pl.pallas_call(
                store_kernel,
                out_shape=outs,
                in_specs=vmem(2),
                out_specs=tuple(hbm(2)),
                scratch_shapes=[pltpu.SemaphoreType.DMA((2,))],
                compiler_params=pltpu.CompilerParams(vmem_limit_bytes=4 << 20),
                name="store",
            )
            return lambda *operands: store_call(*ring_call(*operands))

        return lax.switch(
            branch[0],
            [exchange(index, steps) for index, steps in enumerate(LENGTHS)],
            ends,
            queries,
            key_rows,
            value_rows,
            *local,
            norm_gain.reshape(1, width),
        )

    in_specs = (
        P("seq", "head"),
        P("seq", "head"),
        P("seq", "head"),
        P("head", "seq"),
        P("head"),
        P(),
        P(),
    )
    out_specs = (P("seq", "head"), P("seq", "head", None, None))
    return jax.shard_map(shards, mesh=mesh, in_specs=in_specs, out_specs=out_specs, check_vma=False)
```
